32 devices in a mesh: cell: 2 (over x), seq: 16 (over z, y, core).
Axes of the slice: x: 2, y: 2, z: 4, core: 2. Of those that a mesh axis runs over, the one named last changes fastest.
Arguments:
- queries: bfloat16 [128, 6144], P(('cell', 'seq')), parts along dimension 0, may hold values from -500 to 500
- keys: bfloat16 [256, 128, 1024], P(('cell', 'seq')), parts along dimension 0, may hold values from -6 to 6
- values: bfloat16 [256, 128, 1024], P(('cell', 'seq')), parts along dimension 0, may hold values from -6 to 6
- page_request: int32 [256], P(('cell', 'seq')), parts along dimension 0, may hold values from 0 to 63, as said below
- page_fill: int32 [256], P(('cell', 'seq')), parts along dimension 0, may hold values from 0 to 128
Outputs:
- attended: bfloat16 [128, 6144], P(('cell', 'seq')), parts along dimension 0
The draws below stay inside these ranges and needn't reach their ends.
There are 2 independent parts, one for each index of `cell`. The reference program is written for one: setup_inputs(seed, part) draws one part's arguments, and reference() takes and returns one part's arrays. A program takes and returns all parts, laid end to end along the dimension named above; each array names one. Nothing has to cross between parts.
Inputs may be any that keep to these rules, and one draw needn't show every extreme that they name: `page_request`: every request has at least one page with a live slot. Request r's home is index r // 4 of seq; among one device's pages, the requests of any one home are at most 2 distinct ones, and some device reaches that.
All inputs are finite; a program needn't handle non-finite values.
Results may differ from the reference program's by a relative error of at most 0.0035.
Values may be sent and summed in bfloat16 or wider, within the bound.
A program may use at most 64 MiB of HBM per device.

```python
import jax
import jax.numpy as jnp
from jax import lax

HEADS = 48
KV_HEADS = 8
HEAD_DIM = 128
PAGE = 128
REQ_DEV = 4
PAGE_DEV = 8
GROUP = 6
REQUESTS = 64
PAGES = 128
N_SEQ = 16


def layout(key):
    base = jax.random.fold_in(key, 7)
    pairs = PAGE_DEV // 2
    order = jax.random.permutation(jax.random.fold_in(base, 1), N_SEQ)
    position = jax.random.permutation(jax.random.fold_in(base, 2), N_SEQ)
    rotation = jax.random.randint(jax.random.fold_in(base, 3), (N_SEQ,), 0, REQ_DEV)
    device_ids = jnp.arange(N_SEQ, dtype=jnp.int32)[:, None]
    pair_ids = jnp.arange(pairs, dtype=jnp.int32)[None, :]
    home = order[(position[device_ids] + pair_ids) % N_SEQ]
    first = (pair_ids + rotation[home]) % REQ_DEV
    second = jnp.where(pair_ids % 2 == 0, (first + 1) % REQ_DEV, first)
    owners = home[..., None] * REQ_DEV + jnp.stack([first, second], axis=-1)
    even = jnp.broadcast_to((pair_ids % 2 == 0)[..., None], (N_SEQ, pairs, 2))
    filled = jnp.clip(jax.random.randint(jax.random.fold_in(base, 4), (N_SEQ, pairs, 2), -40, PAGE + 1), 0, PAGE)
    filled = jnp.where(even, jnp.maximum(filled, 1), filled)
    owners = owners.reshape(N_SEQ, PAGE_DEV).astype(jnp.int32)
    filled = filled.reshape(N_SEQ, PAGE_DEV).astype(jnp.int32)
    shuffle_key = jax.random.fold_in(base, 5)

    def shuffle(index):
        return jax.random.permutation(jax.random.fold_in(shuffle_key, index), PAGE_DEV)
    perms = jax.vmap(shuffle)(jnp.arange(N_SEQ, dtype=jnp.int32))
    owners = jnp.take_along_axis(owners, perms, axis=1)
    filled = jnp.take_along_axis(filled, perms, axis=1)
    return (owners.reshape(PAGES), filled.reshape(PAGES))


def draw_page_request(key, part):
    return layout(key)[0]


def draw_page_fill(key, part):
    return layout(key)[1]


def draw_queries(key, part):
    base = jax.random.normal(jax.random.fold_in(key, 11), (REQUESTS, HEADS * HEAD_DIM), jnp.float32)
    base = jnp.clip(base, -6.0, 6.0)
    return base.astype(jnp.bfloat16)


def block_levels(key, dims, shards, least, top_value):
    level = 1.0
    for dim, parts in shards:
        steps = jax.random.uniform(jax.random.fold_in(jax.random.fold_in(key, 6), dim), (parts,), jnp.float32, least / len(shards), top_value / len(shards))
        level = level * jnp.repeat(jnp.exp(steps), dims[dim] // parts).reshape((-1,) + (1,) * (len(dims) - 1 - dim))
    return level


def bell_draw(rng, extent, spread, bound, shards=(), kind=jnp.bfloat16):
    drawn = spread * jax.random.normal(rng, extent, jnp.float32)
    if shards:
        drawn = drawn * block_levels(rng, extent, shards, -0.22, 0.18)
    return jnp.clip(drawn, -bound, bound).astype(kind)


def setup_inputs(seed: int = 0, part: int = 0) -> dict:
    splits = jax.random.split(jax.random.key(seed), 6)
    part_keys = jax.random.split(jax.random.fold_in(splits[5], part), 6)
    queries = draw_queries(jax.random.fold_in(jax.random.fold_in(splits[5], part), 71), part)
    keys = bell_draw(part_keys[1], (PAGES, PAGE, KV_HEADS * HEAD_DIM), 1.0, 6.0, ((0, 16),))
    values = bell_draw(part_keys[2], (PAGES, PAGE, KV_HEADS * HEAD_DIM), 1.0, 6.0, ((0, 16),))
    page_request = draw_page_request(jax.random.fold_in(jax.random.fold_in(splits[5], part), 71), part)
    page_fill = draw_page_fill(jax.random.fold_in(jax.random.fold_in(splits[5], part), 71), part)
    return {"queries": queries, "keys": keys, "values": values, "page_request": page_request, "page_fill": page_fill}


FLOOR = -30000.0


def device_partials(everyone, keys, values, page_request, page_fill):
    pages = keys.shape[0]
    chosen = jnp.take(everyone, page_request, axis=0).reshape(pages, KV_HEADS, GROUP, HEAD_DIM)
    keyed = keys.reshape(pages, PAGE, KV_HEADS, HEAD_DIM)
    valued = values.reshape(pages, PAGE, KV_HEADS, HEAD_DIM)
    scores = jnp.einsum('pkgd,ptkd->pkgt', chosen.astype(jnp.float32), keyed.astype(jnp.float32)) * (HEAD_DIM ** -0.5)
    live = (lax.broadcasted_iota(jnp.int32, (pages, PAGE), 1) < page_fill[:, None])[:, None, None, :]
    page_max = jnp.max(jnp.where(live, scores, FLOOR), axis=3)
    weights = jnp.where(live, jnp.exp(scores - page_max[..., None]), 0.0).astype(jnp.bfloat16)
    page_sum = jnp.sum(weights.astype(jnp.float32), axis=3).reshape(pages, HEADS)
    page_acc = jnp.einsum('pkgt,ptkd->pkgd', weights.astype(jnp.float32), valued.astype(jnp.float32)).reshape(pages, HEADS, HEAD_DIM)
    page_max = page_max.reshape(pages, HEADS)
    member = page_request[None, :] == lax.broadcasted_iota(jnp.int32, (REQUESTS, pages), 0)
    local_max = jnp.max(jnp.where(member[:, :, None], page_max[None], FLOOR), axis=1)
    factor = jnp.where(member[:, :, None], jnp.exp(page_max[None] - local_max[:, None, :]), 0.0)
    local_sum = jnp.sum(factor * page_sum[None], axis=1)
    local_acc = jnp.einsum('rph,phd->rhd', factor, page_acc, precision=lax.Precision.HIGHEST)
    partial_value = (local_acc / jnp.maximum(local_sum, 1.0)[..., None]).astype(jnp.bfloat16)
    return partial_value, local_max, local_sum


def reference(queries, keys, values, page_request, page_fill):
    width = KV_HEADS * HEAD_DIM
    keys_dev = keys.reshape(N_SEQ, PAGE_DEV, PAGE, width)
    values_dev = values.reshape(N_SEQ, PAGE_DEV, PAGE, width)
    request_dev = page_request.reshape(N_SEQ, PAGE_DEV)
    fill_dev = page_fill.reshape(N_SEQ, PAGE_DEV)

    def one_device(items):
        return device_partials(queries, items[0], items[1], items[2], items[3])

    partial_value, local_max, local_sum = lax.map(one_device, (keys_dev, values_dev, request_dev, fill_dev))
    top = jnp.max(local_max, axis=0)
    share = local_sum * jnp.exp(local_max - top[None])

    def accumulate(total, items):
        return total + items[0][..., None] * items[1].astype(jnp.float32), None

    numer, _ = lax.scan(accumulate, jnp.zeros((REQUESTS, HEADS, HEAD_DIM), jnp.float32), (share, partial_value))
    denom = jnp.sum(share, axis=0)
    return (numer / denom[..., None]).reshape(REQUESTS, HEADS * HEAD_DIM).astype(jnp.bfloat16)
```

```python
import functools

import jax
import jax.numpy as jnp
from jax import lax
from jax.experimental import pallas as pl
from jax.experimental.pallas import tpu as pltpu
from jax.sharding import PartitionSpec as P

HEAD_DIM = 128
KV_HEADS = 8
FLOOR = -30000.0
SLOTS = 2


def kernel(
    n, req_ref, fill_ref, q_ref, k_hbm, v_hbm, o_ref,
    kbuf, vbuf, qbuf, acc, pbuf, stat, sdata, sstat, rdata, rstat, leaders,
    k_sem, v_sem, q_recv, q_far, q_pair, q_sib, d_send, d_recv, s_send, s_recv,
):
    pages = k_hbm.shape[0]
    req_dev, width = q_ref.shape
    heads = width // HEAD_DIM
    group = heads // KV_HEADS
    far_n = n // 4
    me = lax.axis_index("seq")

    def remote(src, dst, send, recv, peer):
        return pltpu.make_async_remote_copy(
            src_ref=src, dst_ref=dst, send_sem=send, recv_sem=recv,
            device_id={"seq": peer}, device_id_type=pl.DeviceIdType.MESH,
        )

    barrier = pltpu.get_barrier_semaphore()

    def greet(d, _):
        pl.semaphore_signal(
            barrier, inc=1, device_id={"seq": lax.rem(me + d, n)},
            device_id_type=pl.DeviceIdType.MESH,
        )
        return 0

    lax.fori_loop(1, n, greet, 0)
    for p in range(pages):
        pltpu.make_async_copy(k_hbm.at[p], kbuf.at[p], k_sem.at[p]).start()
    for p in range(pages):
        pltpu.make_async_copy(v_hbm.at[p], vbuf.at[p], v_sem.at[p]).start()

    mine = q_ref[...].astype(jnp.float32)
    qbuf[me] = mine.reshape(req_dev, heads, HEAD_DIM).astype(jnp.bfloat16)
    pl.semaphore_wait(barrier, n - 1)

    far = me // 4
    place = lax.rem(me, 4)
    other = lax.rem(place + 2, 4)
    pair = far * 4 + other
    sibling = me + 1 - 2 * lax.rem(me, 2)

    def far_copy(k, owner, peer):
        return remote(qbuf.at[owner], qbuf.at[owner], q_far.at[k], q_recv.at[owner], peer)

    def pair_copy(k, owner):
        return remote(qbuf.at[owner], qbuf.at[owner], q_pair.at[k], q_recv.at[owner], pair)

    def sib_copy(k, owner):
        return remote(qbuf.at[owner], qbuf.at[owner], q_sib.at[k], q_recv.at[owner], sibling)

    def start_far(k, _):
        far_copy(k, me, lax.rem(far + k, far_n) * 4 + place).start()
        return 0

    lax.fori_loop(1, far_n, start_far, 0)
    pair_copy(0, me).start()
    sib_copy(0, me).start()

    def lead(g, _):
        first = jnp.int32(pages)
        held = jnp.int32(-1)
        for p in reversed(range(pages)):
            hit = req_ref[p] // req_dev == g
            first = jnp.where(hit, p, first)
            held = jnp.where(hit, req_ref[p], held)
        second = jnp.int32(pages)
        for p in reversed(range(pages)):
            hit = jnp.logical_and(req_ref[p] // req_dev == g, req_ref[p] != held)
            second = jnp.where(hit, p, second)
        leaders[SLOTS * g] = first
        leaders[SLOTS * g + 1] = second
        return 0

    lax.fori_loop(0, n, lead, 0)

    def pass_far(k, _):
        owner = lax.rem(far + far_n - k, far_n) * 4 + place
        far_copy(k, owner, owner).wait_recv()
        pair_copy(k, owner).start()
        sib_copy(k, owner).start()
        return 0

    lax.fori_loop(1, far_n, pass_far, 0)

    def pass_pair(k, _):
        owner = lax.rem(far + far_n - k, far_n) * 4 + other
        pair_copy(k, owner).wait_recv()
        sib_copy(far_n + k, owner).start()
        return 0

    lax.fori_loop(0, far_n, pass_pair, 0)

    def wait_sib(k, _):
        owner = 2 * k + lax.rem(sibling, 2)
        sib_copy(k, owner).wait_recv()
        return 0

    lax.fori_loop(0, n // 2, wait_sib, 0)

    lane = lax.broadcasted_iota(jnp.int32, (heads, HEAD_DIM), 1)
    key_head = lax.broadcasted_iota(jnp.int32, (heads, HEAD_DIM), 0) // group
    flat = (heads, HEAD_DIM)
    maxes, sums = [], []
    for p in range(pages):
        r = req_ref[p]
        q = qbuf[r // req_dev, lax.rem(r, req_dev)]
        wide = jnp.concatenate(
            [jnp.where(key_head == k, q, jnp.zeros_like(q)) for k in range(KV_HEADS)], axis=1
        )
        pltpu.make_async_copy(k_hbm.at[p], kbuf.at[p], k_sem.at[p]).wait()
        score = lax.dot_general(
            wide, kbuf[p], (((1,), (1,)), ((), ())), preferred_element_type=jnp.float32
        ) * HEAD_DIM ** (-0.5)
        live = lax.broadcasted_iota(jnp.int32, score.shape, 1) < fill_ref[p]
        top = jnp.max(jnp.where(live, score, FLOOR), axis=1, keepdims=True)
        weight = jnp.where(live, jnp.exp(score - top), 0.0).astype(jnp.bfloat16)
        total = jnp.sum(weight.astype(jnp.float32), axis=1, keepdims=True)
        pltpu.make_async_copy(v_hbm.at[p], vbuf.at[p], v_sem.at[p]).wait()
        mixed = jnp.dot(weight, vbuf[p], preferred_element_type=jnp.float32)
        out = jnp.zeros(flat, jnp.float32)
        for k in range(KV_HEADS):
            out = jnp.where(key_head == k, mixed[:, k * HEAD_DIM:(k + 1) * HEAD_DIM], out)
        acc[p] = out
        maxes.append(jnp.broadcast_to(top, flat))
        sums.append(jnp.broadcast_to(total, flat))

    packed = jnp.zeros(flat, jnp.float32)
    for p in range(pages):
        same = [req_ref[p] == req_ref[q] for q in range(pages)]
        slot_max = jnp.full(flat, FLOOR, jnp.float32)
        for q in range(pages):
            slot_max = jnp.maximum(slot_max, jnp.where(same[q], maxes[q], FLOOR))
        slot_sum = jnp.zeros(flat, jnp.float32)
        slot_acc = jnp.zeros(flat, jnp.float32)
        for q in range(pages):
            factor = jnp.where(same[q], jnp.exp(maxes[q] - slot_max), 0.0)
            slot_sum += factor * sums[q]
            slot_acc += factor * acc[q]
        pbuf[p] = (slot_acc / jnp.maximum(slot_sum, 1.0)).astype(jnp.bfloat16)
        packed = jnp.where(lane == 2 * p, slot_max, packed)
        packed = jnp.where(lane == 2 * p + 1, slot_sum, packed)
    pbuf[pages] = jnp.zeros(flat, jnp.bfloat16)
    turned = jnp.concatenate(
        [packed, jnp.zeros((HEAD_DIM - heads, HEAD_DIM), jnp.float32)], axis=0
    ).T
    row = lax.broadcasted_iota(jnp.int32, (8, HEAD_DIM), 0)
    part = lax.rem(row, 4)
    for p in range(pages):
        local = lax.rem(req_ref[p], req_dev).astype(jnp.float32)
        tile = jnp.where(part == 0, turned[2 * p:2 * p + 1], turned[2 * p + 1:2 * p + 2])
        stat[p] = jnp.where(part >= 2, local, tile)
    stat[pages] = jnp.where(part == 0, FLOOR, jnp.where(part == 1, 0.0, -1.0))

    def build(g, _):
        first = leaders[SLOTS * g]
        second = leaders[SLOTS * g + 1]
        sstat[g] = jnp.where(row < 4, stat[first], stat[second])
        sdata[g, 0] = pbuf[first]
        sdata[g, 1] = pbuf[second]
        return 0

    lax.fori_loop(0, n, build, 0)

    def stat_copy(owner, peer):
        return remote(sstat.at[peer], rstat.at[owner], s_send.at[peer], s_recv.at[owner], peer)

    def data_copy(owner, peer):
        return remote(sdata.at[peer], rdata.at[owner], d_send.at[peer], d_recv.at[owner], peer)

    def send_stat(d, _):
        stat_copy(me, lax.rem(me + d, n)).start()
        return 0

    def send_data(d, _):
        data_copy(me, lax.rem(me + d, n)).start()
        return 0

    lax.fori_loop(1, n, send_stat, 0)
    lax.fori_loop(1, n, send_data, 0)
    rstat[me] = sstat[me]
    rdata[me] = sdata[me]

    def wait_stat(d, _):
        owner = lax.rem(me + n - d, n)
        stat_copy(owner, owner).wait_recv()
        return 0

    lax.fori_loop(1, n, wait_stat, 0)

    rows = 8 * n
    got = rstat[...].reshape(rows, HEAD_DIM)
    got_sum = pltpu.roll(got, rows - 1, 0)
    got_id = pltpu.roll(got, rows - 2, 0)
    got_part = lax.rem(lax.broadcasted_iota(jnp.int32, got.shape, 0), 4)
    real = got_part == 0
    ids = jnp.where(real, got_id, -1.0)
    level = jnp.zeros_like(got)
    for r in range(req_dev):
        hit = ids == r
        best = jnp.max(jnp.where(hit, got, FLOOR), axis=0, keepdims=True)
        level = jnp.where(hit, best, level)
    share = jnp.where(ids >= 0.0, got_sum * jnp.exp(jnp.minimum(got - level, 0.0)), 0.0)
    whole = jnp.ones_like(got)
    for r in range(req_dev):
        hit = ids == r
        denom = jnp.sum(jnp.where(hit, share, 0.0), axis=0, keepdims=True)
        whole = jnp.where(hit, denom, whole)
    table = jnp.where(real, share / whole, got).T[:heads]

    def wait_data(d, _):
        owner = lax.rem(me + n - d, n)
        data_copy(owner, owner).wait_recv()
        return 0

    lax.fori_loop(1, n, wait_data, 0)
    totals = [jnp.zeros((heads // 8, 8, HEAD_DIM), jnp.float32) for _ in range(req_dev)]
    for s in range(n):
        for j in range(SLOTS):
            at = 8 * s + 4 * j
            weight = jnp.broadcast_to(table[:, at:at + 1], flat)
            ident = jnp.broadcast_to(table[:8, at + 2:at + 3], (8, HEAD_DIM))
            term = (weight * rdata[s, j].astype(jnp.float32)).reshape(heads // 8, 8, HEAD_DIM)
            for r in range(req_dev):
                totals[r] += jnp.where((ident == r)[None], term, 0.0)
    for r in range(req_dev):
        o_ref[r] = totals[r].reshape(flat).astype(jnp.bfloat16)

    def done_far(k, _):
        far_copy(k, me, sibling).wait_send()
        pair_copy(k, me).wait_send()
        return 0

    lax.fori_loop(1, far_n, done_far, 0)
    pair_copy(0, me).wait_send()

    def done_sib(k, _):
        sib_copy(k, me).wait_send()
        return 0

    lax.fori_loop(0, n // 2, done_sib, 0)

    def done_out(d, _):
        peer = lax.rem(me + d, n)
        stat_copy(me, peer).wait_send()
        data_copy(me, peer).wait_send()
        return 0

    lax.fori_loop(1, n, done_out, 0)


def body(n, queries, keys, values, page_request, page_fill):
    req_dev, width = queries.shape
    pages, page_len, kv_width = keys.shape
    heads = width // HEAD_DIM
    row = (heads, HEAD_DIM)
    dma = pltpu.SemaphoreType.DMA
    smem = pl.BlockSpec(memory_space=pltpu.SMEM)
    vmem = pl.BlockSpec(memory_space=pltpu.VMEM)
    hbm = pl.BlockSpec(memory_space=pl.ANY)
    out = pl.pallas_call(
        functools.partial(kernel, n),
        out_shape=jax.ShapeDtypeStruct((req_dev,) + row, jnp.bfloat16),
        in_specs=[smem, smem, vmem, hbm, hbm],
        out_specs=vmem,
        scratch_shapes=[
            pltpu.VMEM((pages, page_len, kv_width), jnp.bfloat16),
            pltpu.VMEM((pages, page_len, kv_width), jnp.bfloat16),
            pltpu.VMEM((n, req_dev) + row, jnp.bfloat16),
            pltpu.VMEM((pages,) + row, jnp.float32),
            pltpu.VMEM((pages + 1,) + row, jnp.bfloat16),
            pltpu.VMEM((pages + 1, 8, HEAD_DIM), jnp.float32),
            pltpu.VMEM((n, SLOTS) + row, jnp.bfloat16),
            pltpu.VMEM((n, 8, HEAD_DIM), jnp.float32),
            pltpu.VMEM((n, SLOTS) + row, jnp.bfloat16),
            pltpu.VMEM((n, 8, HEAD_DIM), jnp.float32),
            pltpu.SMEM((SLOTS * n,), jnp.int32),
            dma((pages,)), dma((pages,)), dma((n,)), dma((n // 4,)), dma((n // 4,)),
            dma((n // 2,)), dma((n,)), dma((n,)), dma((n,)), dma((n,)),
        ],
        compiler_params=pltpu.CompilerParams(collective_id=0, has_side_effects=True),
    )(page_request, page_fill, queries, keys, values)
    return out.reshape(req_dev, width)


def solution(mesh):
    rows = P(("cell", "seq"))
    return jax.shard_map(
        functools.partial(body, mesh.shape["seq"]), mesh=mesh,
        in_specs=(rows, rows, rows, rows, rows), out_specs=rows, check_vma=False,
    )
```

```python
import functools

import jax
import jax.numpy as jnp
from jax import lax
from jax.experimental import pallas as pl
from jax.experimental.pallas import tpu as pltpu
from jax.sharding import PartitionSpec as P

HEAD_DIM = 128
KV_HEADS = 8
FLOOR = -30000.0
SLOTS = 2
PARTS = 2


def kernel(
    n, req_ref, fill_ref, q_ref, k_hbm, v_hbm, o_ref,
    kbuf, vbuf, qbuf0, qbuf1, acc, pbuf, stat, sdata, sstat, rdata, rstat, leaders,
    k_sem, v_sem, q_recv, q_far, q_pair, q_sib, d_send, d_recv, s_send, s_recv,
):
    pages = k_hbm.shape[0]
    req_dev, width = q_ref.shape
    heads = width // HEAD_DIM
    group = heads // KV_HEADS
    part_heads = heads // PARTS
    part_keys = KV_HEADS // PARTS
    span = part_keys * HEAD_DIM
    far_n = n // 4
    me = lax.axis_index("seq")
    qbuf = (qbuf0, qbuf1)

    def remote(src, dst, send, recv, peer):
        return pltpu.make_async_remote_copy(
            src_ref=src, dst_ref=dst, send_sem=send, recv_sem=recv,
            device_id={"seq": peer}, device_id_type=pl.DeviceIdType.MESH,
        )

    barrier = pltpu.get_barrier_semaphore()

    def greet(d, _):
        pl.semaphore_signal(
            barrier, inc=1, device_id={"seq": lax.rem(me + d, n)},
            device_id_type=pl.DeviceIdType.MESH,
        )
        return 0

    lax.fori_loop(1, n, greet, 0)
    for p in range(pages):
        pltpu.make_async_copy(k_hbm.at[p], kbuf.at[p], k_sem.at[p]).start()
    for p in range(pages):
        pltpu.make_async_copy(v_hbm.at[p], vbuf.at[p], v_sem.at[p]).start()

    mine = q_ref[...].astype(jnp.float32)
    mine = mine.reshape(req_dev, heads, HEAD_DIM)
    for h in range(PARTS):
        qbuf[h][me] = mine[:, h * part_heads:(h + 1) * part_heads].astype(jnp.bfloat16)
    pl.semaphore_wait(barrier, n - 1)

    far = me // 4
    place = lax.rem(me, 4)
    other = lax.rem(place + 2, 4)
    pair = far * 4 + other
    sibling = me + 1 - 2 * lax.rem(me, 2)

    def far_copy(h, k, owner, peer):
        block = qbuf[h].at[owner]
        return remote(block, block, q_far.at[h, k], q_recv.at[h, owner], peer)

    def pair_copy(h, k, owner):
        block = qbuf[h].at[owner]
        return remote(block, block, q_pair.at[h, k], q_recv.at[h, owner], pair)

    def sib_copy(h, k, owner):
        block = qbuf[h].at[owner]
        return remote(block, block, q_sib.at[h, k], q_recv.at[h, owner], sibling)

    for h in range(PARTS):
        def start_far(k, _):
            far_copy(h, k, me, lax.rem(far + k, far_n) * 4 + place).start()
            return 0

        lax.fori_loop(1, far_n, start_far, 0)
        pair_copy(h, 0, me).start()
        sib_copy(h, 0, me).start()

    def lead(g, _):
        first = jnp.int32(pages)
        held = jnp.int32(-1)
        for p in reversed(range(pages)):
            hit = req_ref[p] // req_dev == g
            first = jnp.where(hit, p, first)
            held = jnp.where(hit, req_ref[p], held)
        second = jnp.int32(pages)
        for p in reversed(range(pages)):
            hit = jnp.logical_and(req_ref[p] // req_dev == g, req_ref[p] != held)
            second = jnp.where(hit, p, second)
        leaders[SLOTS * g] = first
        leaders[SLOTS * g + 1] = second
        return 0

    lax.fori_loop(0, n, lead, 0)

    def pass_far(h):
        def step(k, _):
            owner = lax.rem(far + far_n - k, far_n) * 4 + place
            far_copy(h, k, owner, owner).wait_recv()
            pair_copy(h, k, owner).start()
            sib_copy(h, k, owner).start()
            return 0

        lax.fori_loop(1, far_n, step, 0)

    def pass_pair(h):
        def step(k, _):
            owner = lax.rem(far + far_n - k, far_n) * 4 + other
            pair_copy(h, k, owner).wait_recv()
            sib_copy(h, far_n + k, owner).start()
            return 0

        lax.fori_loop(0, far_n, step, 0)

    def wait_sib(h):
        def step(k, _):
            sib_copy(h, k, 2 * k + lax.rem(sibling, 2)).wait_recv()
            return 0

        lax.fori_loop(0, n // 2, step, 0)

    flat = (part_heads, HEAD_DIM)
    lane = lax.broadcasted_iota(jnp.int32, flat, 1)
    key_head = lax.broadcasted_iota(jnp.int32, flat, 0) // group

    def attend(h, p):
        r = req_ref[p]
        q = qbuf[h][r // req_dev, lax.rem(r, req_dev)]
        wide = jnp.concatenate(
            [jnp.where(key_head == k, q, jnp.zeros_like(q)) for k in range(part_keys)], axis=1
        )
        if h == 0:
            pltpu.make_async_copy(k_hbm.at[p], kbuf.at[p], k_sem.at[p]).wait()
            pltpu.make_async_copy(v_hbm.at[p], vbuf.at[p], v_sem.at[p]).wait()
        score = lax.dot_general(
            wide, kbuf[p, :, h * span:(h + 1) * span], (((1,), (1,)), ((), ())),
            preferred_element_type=jnp.float32,
        ) * HEAD_DIM ** (-0.5)
        live = lax.broadcasted_iota(jnp.int32, score.shape, 1) < fill_ref[p]
        top = jnp.max(jnp.where(live, score, FLOOR), axis=1, keepdims=True)
        weight = jnp.where(live, jnp.exp(score - top), 0.0).astype(jnp.bfloat16)
        total = jnp.sum(weight.astype(jnp.float32), axis=1, keepdims=True)
        mixed = jnp.dot(
            weight, vbuf[p, :, h * span:(h + 1) * span], preferred_element_type=jnp.float32
        )
        out = jnp.zeros(flat, jnp.float32)
        for k in range(part_keys):
            out = jnp.where(key_head == k, mixed[:, k * HEAD_DIM:(k + 1) * HEAD_DIM], out)
        acc[h, p] = out
        return jnp.broadcast_to(top, flat), jnp.broadcast_to(total, flat)

    row = lax.broadcasted_iota(jnp.int32, (8, HEAD_DIM), 0)
    part = lax.rem(row, 4)

    def merge(h, maxes, sums):
        packed = jnp.zeros(flat, jnp.float32)
        for p in range(pages):
            same = [req_ref[p] == req_ref[q] for q in range(pages)]
            slot_max = jnp.full(flat, FLOOR, jnp.float32)
            for q in range(pages):
                slot_max = jnp.maximum(slot_max, jnp.where(same[q], maxes[q], FLOOR))
            slot_sum = jnp.zeros(flat, jnp.float32)
            slot_acc = jnp.zeros(flat, jnp.float32)
            for q in range(pages):
                factor = jnp.where(same[q], jnp.exp(maxes[q] - slot_max), 0.0)
                slot_sum += factor * sums[q]
                slot_acc += factor * acc[h, q]
            pbuf[h, p] = (slot_acc / jnp.maximum(slot_sum, 1.0)).astype(jnp.bfloat16)
            packed = jnp.where(lane == 2 * p, slot_max, packed)
            packed = jnp.where(lane == 2 * p + 1, slot_sum, packed)
        pbuf[h, pages] = jnp.zeros(flat, jnp.bfloat16)
        turned = jnp.concatenate(
            [packed, jnp.zeros((HEAD_DIM - part_heads, HEAD_DIM), jnp.float32)], axis=0
        ).T
        for p in range(pages):
            local = lax.rem(req_ref[p], req_dev).astype(jnp.float32)
            tile = jnp.where(part == 0, turned[2 * p:2 * p + 1], turned[2 * p + 1:2 * p + 2])
            stat[h, p] = jnp.where(part >= 2, local, tile)
        stat[h, pages] = jnp.where(part == 0, FLOOR, jnp.where(part == 1, 0.0, -1.0))

        def build(g, _):
            first = leaders[SLOTS * g]
            second = leaders[SLOTS * g + 1]
            sstat[h, g] = jnp.where(row < 4, stat[h, first], stat[h, second])
            sdata[h, g, 0] = pbuf[h, first]
            sdata[h, g, 1] = pbuf[h, second]
            return 0

        lax.fori_loop(0, n, build, 0)

    def stat_copy(h, owner, peer):
        return remote(
            sstat.at[h, peer], rstat.at[h, owner], s_send.at[h, peer], s_recv.at[h, owner], peer
        )

    def data_copy(h, owner, peer):
        return remote(
            sdata.at[h, peer], rdata.at[h, owner], d_send.at[h, peer], d_recv.at[h, owner], peer
        )

    def send(h):
        def step(d, _):
            stat_copy(h, me, lax.rem(me + d, n)).start()
            data_copy(h, me, lax.rem(me + d, n)).start()
            return 0

        lax.fori_loop(1, n, step, 0)
        rstat[h, me] = sstat[h, me]
        rdata[h, me] = sdata[h, me]

    def combine(h):
        def wait_stat(d, _):
            owner = lax.rem(me + n - d, n)
            stat_copy(h, owner, owner).wait_recv()
            return 0

        lax.fori_loop(1, n, wait_stat, 0)
        rows = 8 * n
        got = rstat[h].reshape(rows, HEAD_DIM)
        got_sum = pltpu.roll(got, rows - 1, 0)
        got_id = pltpu.roll(got, rows - 2, 0)
        got_part = lax.rem(lax.broadcasted_iota(jnp.int32, got.shape, 0), 4)
        real = got_part == 0
        ids = jnp.where(real, got_id, -1.0)
        level = jnp.zeros_like(got)
        for r in range(req_dev):
            hit = ids == r
            best = jnp.max(jnp.where(hit, got, FLOOR), axis=0, keepdims=True)
            level = jnp.where(hit, best, level)
        share = jnp.where(ids >= 0.0, got_sum * jnp.exp(jnp.minimum(got - level, 0.0)), 0.0)
        whole = jnp.ones_like(got)
        for r in range(req_dev):
            hit = ids == r
            denom = jnp.sum(jnp.where(hit, share, 0.0), axis=0, keepdims=True)
            whole = jnp.where(hit, denom, whole)
        table = jnp.where(real, share / whole, got).T[:part_heads]

        def wait_data(d, _):
            owner = lax.rem(me + n - d, n)
            data_copy(h, owner, owner).wait_recv()
            return 0

        lax.fori_loop(1, n, wait_data, 0)
        totals = [jnp.zeros((part_heads // 8, 8, HEAD_DIM), jnp.float32) for _ in range(req_dev)]
        for s in range(n):
            for j in range(SLOTS):
                at = 8 * s + 4 * j
                weight = jnp.broadcast_to(table[:, at:at + 1], flat)
                ident = jnp.broadcast_to(table[:8, at + 2:at + 3], (8, HEAD_DIM))
                term = (weight * rdata[h, s, j].astype(jnp.float32)).reshape(part_heads // 8, 8, HEAD_DIM)
                for r in range(req_dev):
                    totals[r] += jnp.where((ident == r)[None], term, 0.0)
        return [total.reshape(flat) for total in totals]

    pass_far(0)
    pass_pair(0)
    pass_far(1)
    wait_sib(0)
    found = [attend(0, p) for p in range(pages // 2)]
    pass_pair(1)
    found += [attend(0, p) for p in range(pages // 2, pages)]
    merge(0, [f[0] for f in found], [f[1] for f in found])
    send(0)
    wait_sib(1)
    found = [attend(1, p) for p in range(pages)]
    merge(1, [f[0] for f in found], [f[1] for f in found])
    send(1)
    merged = [combine(h) for h in range(PARTS)]
    for r in range(req_dev):
        o_ref[r] = jnp.concatenate([m[r] for m in merged], axis=0).astype(jnp.bfloat16)

    for h in range(PARTS):
        def done_far(k, _):
            far_copy(h, k, me, sibling).wait_send()
            pair_copy(h, k, me).wait_send()
            return 0

        def done_sib(k, _):
            sib_copy(h, k, me).wait_send()
            return 0

        def done_out(d, _):
            peer = lax.rem(me + d, n)
            stat_copy(h, me, peer).wait_send()
            data_copy(h, me, peer).wait_send()
            return 0

        lax.fori_loop(1, far_n, done_far, 0)
        pair_copy(h, 0, me).wait_send()
        lax.fori_loop(0, n // 2, done_sib, 0)
        lax.fori_loop(1, n, done_out, 0)


def body(n, queries, keys, values, page_request, page_fill):
    req_dev, width = queries.shape
    pages, page_len, kv_width = keys.shape
    heads = width // HEAD_DIM
    row = (heads, HEAD_DIM)
    part = (heads // PARTS, HEAD_DIM)
    dma = pltpu.SemaphoreType.DMA
    smem = pl.BlockSpec(memory_space=pltpu.SMEM)
    vmem = pl.BlockSpec(memory_space=pltpu.VMEM)
    hbm = pl.BlockSpec(memory_space=pl.ANY)
    out = pl.pallas_call(
        functools.partial(kernel, n),
        out_shape=jax.ShapeDtypeStruct((req_dev,) + row, jnp.bfloat16),
        in_specs=[smem, smem, vmem, hbm, hbm],
        out_specs=vmem,
        scratch_shapes=[
            pltpu.VMEM((pages, page_len, kv_width), jnp.bfloat16),
            pltpu.VMEM((pages, page_len, kv_width), jnp.bfloat16),
            pltpu.VMEM((n, req_dev) + part, jnp.bfloat16),
            pltpu.VMEM((n, req_dev) + part, jnp.bfloat16),
            pltpu.VMEM((PARTS, pages) + part, jnp.float32),
            pltpu.VMEM((PARTS, pages + 1) + part, jnp.bfloat16),
            pltpu.VMEM((PARTS, pages + 1, 8, HEAD_DIM), jnp.float32),
            pltpu.VMEM((PARTS, n, SLOTS) + part, jnp.bfloat16),
            pltpu.VMEM((PARTS, n, 8, HEAD_DIM), jnp.float32),
            pltpu.VMEM((PARTS, n, SLOTS) + part, jnp.bfloat16),
            pltpu.VMEM((PARTS, n, 8, HEAD_DIM), jnp.float32),
            pltpu.SMEM((SLOTS * n,), jnp.int32),
            dma((pages,)), dma((pages,)), dma((PARTS, n)), dma((PARTS, n // 4)),
            dma((PARTS, n // 4)), dma((PARTS, n // 2)), dma((PARTS, n)), dma((PARTS, n)),
            dma((PARTS, n)), dma((PARTS, n)),
        ],
        compiler_params=pltpu.CompilerParams(collective_id=0, has_side_effects=True),
    )(page_request, page_fill, queries, keys, values)
    return out.reshape(req_dev, width)


def solution(mesh):
    rows = P(("cell", "seq"))
    return jax.shard_map(
        functools.partial(body, mesh.shape["seq"]), mesh=mesh,
        in_specs=(rows, rows, rows, rows, rows), out_specs=rows, check_vma=False,
    )
```

```python
import functools

import jax
import jax.numpy as jnp
from jax import lax
from jax.experimental import pallas as pl
from jax.experimental.pallas import tpu as pltpu
from jax.sharding import PartitionSpec as P

HEAD_DIM = 128
KV_HEADS = 8
FLOOR = -30000.0
SLOTS = 2


def kernel(
    n, req_ref, fill_ref, q_ref, k_hbm, v_hbm, o_ref,
    kbuf, vbuf, qbuf, acc, pbuf, stat, sdata, sstat, rdata, rstat, leaders,
    k_sem, v_sem, q_recv, q_far, q_pair, q_sib, d_send, d_recv, s_send, s_recv,
):
    pages = k_hbm.shape[0]
    req_dev, width = q_ref.shape
    heads = width // HEAD_DIM
    group = heads // KV_HEADS
    far_n = n // 4
    me = lax.axis_index("seq")

    def remote(src, dst, send, recv, peer):
        return pltpu.make_async_remote_copy(
            src_ref=src, dst_ref=dst, send_sem=send, recv_sem=recv,
            device_id={"seq": peer}, device_id_type=pl.DeviceIdType.MESH,
        )

    barrier = pltpu.get_barrier_semaphore()

    far = me // 4
    place = lax.rem(me, 4)
    other = lax.rem(place + 2, 4)
    pair = far * 4 + other
    sibling = me + 1 - 2 * lax.rem(me, 2)

    def greet(peer):
        pl.semaphore_signal(
            barrier, inc=1, device_id={"seq": peer}, device_id_type=pl.DeviceIdType.MESH
        )

    def greet_far(k, _):
        greet(lax.rem(far + k, far_n) * 4 + place)
        return 0

    lax.fori_loop(1, far_n, greet_far, 0)
    greet(pair)
    greet(sibling)
    for p in range(pages):
        pltpu.make_async_copy(k_hbm.at[p], kbuf.at[p], k_sem.at[p]).start()
    for p in range(pages):
        pltpu.make_async_copy(v_hbm.at[p], vbuf.at[p], v_sem.at[p]).start()

    mine = q_ref[...].astype(jnp.float32)
    qbuf[me] = mine.reshape(req_dev, heads, HEAD_DIM).astype(jnp.bfloat16)
    pl.semaphore_wait(barrier, far_n + 1)

    def far_copy(k, owner, peer):
        return remote(qbuf.at[owner], qbuf.at[owner], q_far.at[k], q_recv.at[owner], peer)

    def pair_copy(k, owner):
        return remote(qbuf.at[owner], qbuf.at[owner], q_pair.at[k], q_recv.at[owner], pair)

    def sib_copy(k, owner):
        return remote(qbuf.at[owner], qbuf.at[owner], q_sib.at[k], q_recv.at[owner], sibling)

    def start_far(k, _):
        far_copy(k, me, lax.rem(far + k, far_n) * 4 + place).start()
        return 0

    lax.fori_loop(1, far_n, start_far, 0)
    pair_copy(0, me).start()
    sib_copy(0, me).start()

    def lead(g, _):
        first = jnp.int32(pages)
        held = jnp.int32(-1)
        for p in reversed(range(pages)):
            hit = req_ref[p] // req_dev == g
            first = jnp.where(hit, p, first)
            held = jnp.where(hit, req_ref[p], held)
        second = jnp.int32(pages)
        for p in reversed(range(pages)):
            hit = jnp.logical_and(req_ref[p] // req_dev == g, req_ref[p] != held)
            second = jnp.where(hit, p, second)
        leaders[SLOTS * g] = first
        leaders[SLOTS * g + 1] = second
        return 0

    lax.fori_loop(0, n, lead, 0)

    def pass_far(k, _):
        owner = lax.rem(far + far_n - k, far_n) * 4 + place
        far_copy(k, owner, owner).wait_recv()
        pair_copy(k, owner).start()
        sib_copy(k, owner).start()
        return 0

    lax.fori_loop(1, far_n, pass_far, 0)

    def pass_pair(k, _):
        owner = lax.rem(far + far_n - k, far_n) * 4 + other
        pair_copy(k, owner).wait_recv()
        sib_copy(far_n + k, owner).start()
        return 0

    lax.fori_loop(0, far_n, pass_pair, 0)

    def wait_sib(k, _):
        owner = 2 * k + lax.rem(sibling, 2)
        sib_copy(k, owner).wait_recv()
        return 0

    lax.fori_loop(0, n // 2, wait_sib, 0)

    for p in range(pages):
        pltpu.make_async_copy(k_hbm.at[p], kbuf.at[p], k_sem.at[p]).wait()
        pltpu.make_async_copy(v_hbm.at[p], vbuf.at[p], v_sem.at[p]).wait()
    lane = lax.broadcasted_iota(jnp.int32, (heads, HEAD_DIM), 1)
    key_head = lax.broadcasted_iota(jnp.int32, (heads, HEAD_DIM), 0) // group
    flat = (heads, HEAD_DIM)
    maxes, sums = [], []
    for p in range(pages):
        r = req_ref[p]
        q = qbuf[r // req_dev, lax.rem(r, req_dev)]
        wide = jnp.concatenate(
            [jnp.where(key_head == k, q, jnp.zeros_like(q)) for k in range(KV_HEADS)], axis=1
        )
        score = lax.dot_general(
            wide, kbuf[p], (((1,), (1,)), ((), ())), preferred_element_type=jnp.float32
        ) * HEAD_DIM ** (-0.5)
        live = lax.broadcasted_iota(jnp.int32, score.shape, 1) < fill_ref[p]
        top = jnp.max(jnp.where(live, score, FLOOR), axis=1, keepdims=True)
        weight = jnp.where(live, jnp.exp(score - top), 0.0).astype(jnp.bfloat16)
        total = jnp.sum(weight.astype(jnp.float32), axis=1, keepdims=True)
        mixed = jnp.dot(weight, vbuf[p], preferred_element_type=jnp.float32)
        out = jnp.zeros(flat, jnp.float32)
        for k in range(KV_HEADS):
            out = jnp.where(key_head == k, mixed[:, k * HEAD_DIM:(k + 1) * HEAD_DIM], out)
        acc[p] = out
        maxes.append(jnp.broadcast_to(top, flat))
        sums.append(jnp.broadcast_to(total, flat))

    packed = jnp.zeros(flat, jnp.float32)
    for p in range(pages):
        same = [req_ref[p] == req_ref[q] for q in range(pages)]
        slot_max = jnp.full(flat, FLOOR, jnp.float32)
        for q in range(pages):
            slot_max = jnp.maximum(slot_max, jnp.where(same[q], maxes[q], FLOOR))
        slot_sum = jnp.zeros(flat, jnp.float32)
        slot_acc = jnp.zeros(flat, jnp.float32)
        for q in range(pages):
            factor = jnp.where(same[q], jnp.exp(maxes[q] - slot_max), 0.0)
            slot_sum += factor * sums[q]
            slot_acc += factor * acc[q]
        pbuf[p] = (slot_acc / jnp.maximum(slot_sum, 1.0)).astype(jnp.bfloat16)
        packed = jnp.where(lane == 2 * p, slot_max, packed)
        packed = jnp.where(lane == 2 * p + 1, slot_sum, packed)
    pbuf[pages] = jnp.zeros(flat, jnp.bfloat16)
    turned = jnp.concatenate(
        [packed, jnp.zeros((HEAD_DIM - heads, HEAD_DIM), jnp.float32)], axis=0
    ).T
    row = lax.broadcasted_iota(jnp.int32, (8, HEAD_DIM), 0)
    part = lax.rem(row, 4)
    for p in range(pages):
        local = lax.rem(req_ref[p], req_dev).astype(jnp.float32)
        tile = jnp.where(part == 0, turned[2 * p:2 * p + 1], turned[2 * p + 1:2 * p + 2])
        stat[p] = jnp.where(part >= 2, local, tile)
    stat[pages] = jnp.where(part == 0, FLOOR, jnp.where(part == 1, 0.0, -1.0))

    def build(g, _):
        first = leaders[SLOTS * g]
        second = leaders[SLOTS * g + 1]
        sstat[g] = jnp.where(row < 4, stat[first], stat[second])
        sdata[g, 0] = pbuf[first]
        sdata[g, 1] = pbuf[second]
        return 0

    lax.fori_loop(0, n, build, 0)

    def stat_copy(owner, peer):
        return remote(sstat.at[peer], rstat.at[owner], s_send.at[peer], s_recv.at[owner], peer)

    def data_copy(owner, peer):
        return remote(sdata.at[peer], rdata.at[owner], d_send.at[peer], d_recv.at[owner], peer)

    def send_stat(d, _):
        stat_copy(me, lax.rem(me + d, n)).start()
        return 0

    def send_data(d, _):
        data_copy(me, lax.rem(me + d, n)).start()
        return 0

    lax.fori_loop(1, n, send_stat, 0)
    lax.fori_loop(1, n, send_data, 0)
    rstat[me] = sstat[me]
    rdata[me] = sdata[me]

    def wait_stat(d, _):
        owner = lax.rem(me + n - d, n)
        stat_copy(owner, owner).wait_recv()
        return 0

    lax.fori_loop(1, n, wait_stat, 0)

    rows = 8 * n
    got = rstat[...].reshape(rows, HEAD_DIM)
    got_sum = pltpu.roll(got, rows - 1, 0)
    got_id = pltpu.roll(got, rows - 2, 0)
    got_part = lax.rem(lax.broadcasted_iota(jnp.int32, got.shape, 0), 4)
    real = got_part == 0
    ids = jnp.where(real, got_id, -1.0)
    level = jnp.zeros_like(got)
    for r in range(req_dev):
        hit = ids == r
        best = jnp.max(jnp.where(hit, got, FLOOR), axis=0, keepdims=True)
        level = jnp.where(hit, best, level)
    share = jnp.where(ids >= 0.0, got_sum * jnp.exp(jnp.minimum(got - level, 0.0)), 0.0)
    whole = jnp.ones_like(got)
    for r in range(req_dev):
        hit = ids == r
        denom = jnp.sum(jnp.where(hit, share, 0.0), axis=0, keepdims=True)
        whole = jnp.where(hit, denom, whole)
    table = jnp.where(real, share / whole, got).T[:heads]

    def wait_data(d, _):
        owner = lax.rem(me + n - d, n)
        data_copy(owner, owner).wait_recv()
        return 0

    lax.fori_loop(1, n, wait_data, 0)
    totals = [jnp.zeros((heads // 8, 8, HEAD_DIM), jnp.float32) for _ in range(req_dev)]
    for s in range(n):
        for j in range(SLOTS):
            at = 8 * s + 4 * j
            weight = jnp.broadcast_to(table[:, at:at + 1], flat)
            ident = jnp.broadcast_to(table[:8, at + 2:at + 3], (8, HEAD_DIM))
            term = (weight * rdata[s, j].astype(jnp.float32)).reshape(heads // 8, 8, HEAD_DIM)
            for r in range(req_dev):
                totals[r] += jnp.where((ident == r)[None], term, 0.0)
    for r in range(req_dev):
        o_ref[r] = totals[r].reshape(flat).astype(jnp.bfloat16)

    def done_far(k, _):
        far_copy(k, me, sibling).wait_send()
        pair_copy(k, me).wait_send()
        return 0

    lax.fori_loop(1, far_n, done_far, 0)
    pair_copy(0, me).wait_send()

    def done_sib(k, _):
        sib_copy(k, me).wait_send()
        return 0

    lax.fori_loop(0, n // 2, done_sib, 0)

    def done_out(d, _):
        peer = lax.rem(me + d, n)
        stat_copy(me, peer).wait_send()
        data_copy(me, peer).wait_send()
        return 0

    lax.fori_loop(1, n, done_out, 0)


def body(n, queries, keys, values, page_request, page_fill):
    req_dev, width = queries.shape
    pages, page_len, kv_width = keys.shape
    heads = width // HEAD_DIM
    row = (heads, HEAD_DIM)
    dma = pltpu.SemaphoreType.DMA
    smem = pl.BlockSpec(memory_space=pltpu.SMEM)
    vmem = pl.BlockSpec(memory_space=pltpu.VMEM)
    hbm = pl.BlockSpec(memory_space=pl.ANY)
    out = pl.pallas_call(
        functools.partial(kernel, n),
        out_shape=jax.ShapeDtypeStruct((req_dev,) + row, jnp.bfloat16),
        in_specs=[smem, smem, vmem, hbm, hbm],
        out_specs=vmem,
        scratch_shapes=[
            pltpu.VMEM((pages, page_len, kv_width), jnp.bfloat16),
            pltpu.VMEM((pages, page_len, kv_width), jnp.bfloat16),
            pltpu.VMEM((n, req_dev) + row, jnp.bfloat16),
            pltpu.VMEM((pages,) + row, jnp.float32),
            pltpu.VMEM((pages + 1,) + row, jnp.bfloat16),
            pltpu.VMEM((pages + 1, 8, HEAD_DIM), jnp.float32),
            pltpu.VMEM((n, SLOTS) + row, jnp.bfloat16),
            pltpu.VMEM((n, 8, HEAD_DIM), jnp.float32),
            pltpu.VMEM((n, SLOTS) + row, jnp.bfloat16),
            pltpu.VMEM((n, 8, HEAD_DIM), jnp.float32),
            pltpu.SMEM((SLOTS * n,), jnp.int32),
            dma((pages,)), dma((pages,)), dma((n,)), dma((n // 4,)), dma((n // 4,)),
            dma((n // 2,)), dma((n,)), dma((n,)), dma((n,)), dma((n,)),
        ],
        compiler_params=pltpu.CompilerParams(collective_id=0, has_side_effects=True),
    )(page_request, page_fill, queries, keys, values)
    return out.reshape(req_dev, width)


def solution(mesh):
    rows = P(("cell", "seq"))
    return jax.shard_map(
        functools.partial(body, mesh.shape["seq"]), mesh=mesh,
        in_specs=(rows, rows, rows, rows, rows), out_specs=rows, check_vma=False,
    )
```

```python
import functools

import jax
import jax.numpy as jnp
from jax import lax
from jax.experimental import pallas as pl
from jax.experimental.pallas import tpu as pltpu
from jax.sharding import PartitionSpec as P

HEAD_DIM = 128
KV_HEADS = 8
FLOOR = -30000.0
SLOTS = 2


def kernel(
    n, req_ref, fill_ref, q_ref, k_hbm, v_hbm, o_ref,
    kbuf, vbuf, qbuf, acc, pbuf, stat, sdata, sstat, rdata, rstat, leaders,
    k_sem, v_sem, q_recv, q_far, q_pair, q_sib, d_send, d_recv, s_send, s_recv,
):
    pages = k_hbm.shape[0]
    req_dev, width = q_ref.shape
    heads = width // HEAD_DIM
    group = heads // KV_HEADS
    far_n = n // 4
    me = lax.axis_index("seq")

    def remote(src, dst, send, recv, peer):
        return pltpu.make_async_remote_copy(
            src_ref=src, dst_ref=dst, send_sem=send, recv_sem=recv,
            device_id={"seq": peer}, device_id_type=pl.DeviceIdType.MESH,
        )

    barrier = pltpu.get_barrier_semaphore()

    far = me // 4
    place = lax.rem(me, 4)
    other = lax.rem(place + 2, 4)
    pair = far * 4 + other
    sibling = me + 1 - 2 * lax.rem(me, 2)

    def greet(peer):
        pl.semaphore_signal(
            barrier, inc=1, device_id={"seq": peer}, device_id_type=pl.DeviceIdType.MESH
        )

    def greet_far(k, _):
        greet(lax.rem(far + k, far_n) * 4 + place)
        return 0

    lax.fori_loop(1, far_n, greet_far, 0)
    greet(pair)
    greet(sibling)
    for p in range(pages):
        pltpu.make_async_copy(k_hbm.at[p], kbuf.at[p], k_sem.at[p]).start()
    for p in range(pages):
        pltpu.make_async_copy(v_hbm.at[p], vbuf.at[p], v_sem.at[p]).start()

    mine = q_ref[...].astype(jnp.float32)
    qbuf[me] = mine.reshape(req_dev, heads, HEAD_DIM).astype(jnp.bfloat16)
    pl.semaphore_wait(barrier, far_n + 1)

    def far_copy(k, owner, peer):
        return remote(qbuf.at[owner], qbuf.at[owner], q_far.at[k], q_recv.at[owner], peer)

    def pair_copy(k, owner):
        return remote(qbuf.at[owner], qbuf.at[owner], q_pair.at[k], q_recv.at[owner], pair)

    def sib_copy(k, owner):
        return remote(qbuf.at[owner], qbuf.at[owner], q_sib.at[k], q_recv.at[owner], sibling)

    def start_far(k, _):
        far_copy(k, me, lax.rem(far + k, far_n) * 4 + place).start()
        return 0

    lax.fori_loop(1, far_n, start_far, 0)
    pair_copy(0, me).start()
    sib_copy(0, me).start()

    def lead(g, _):
        first = jnp.int32(pages)
        held = jnp.int32(-1)
        for p in reversed(range(pages)):
            hit = req_ref[p] // req_dev == g
            first = jnp.where(hit, p, first)
            held = jnp.where(hit, req_ref[p], held)
        second = jnp.int32(pages)
        for p in reversed(range(pages)):
            hit = jnp.logical_and(req_ref[p] // req_dev == g, req_ref[p] != held)
            second = jnp.where(hit, p, second)
        leaders[SLOTS * g] = first
        leaders[SLOTS * g + 1] = second
        return 0

    lax.fori_loop(0, n, lead, 0)

    def pass_far(k, _):
        owner = lax.rem(far + far_n - k, far_n) * 4 + place
        far_copy(k, owner, owner).wait_recv()
        pair_copy(k, owner).start()
        sib_copy(k, owner).start()
        return 0

    lax.fori_loop(1, far_n, pass_far, 0)

    def pass_pair(k, _):
        owner = lax.rem(far + far_n - k, far_n) * 4 + other
        pair_copy(k, owner).wait_recv()
        sib_copy(far_n + k, owner).start()
        return 0

    lax.fori_loop(0, far_n, pass_pair, 0)

    def wait_sib(k, _):
        owner = 2 * k + lax.rem(sibling, 2)
        sib_copy(k, owner).wait_recv()
        return 0

    lax.fori_loop(0, n // 2, wait_sib, 0)

    for p in range(pages):
        pltpu.make_async_copy(k_hbm.at[p], kbuf.at[p], k_sem.at[p]).wait()
        pltpu.make_async_copy(v_hbm.at[p], vbuf.at[p], v_sem.at[p]).wait()
    lane = lax.broadcasted_iota(jnp.int32, (heads, HEAD_DIM), 1)
    key_head = lax.broadcasted_iota(jnp.int32, (heads, HEAD_DIM), 0) // group
    flat = (heads, HEAD_DIM)
    maxes, sums = [], []
    for p in range(pages):
        r = req_ref[p]
        q = qbuf[r // req_dev, lax.rem(r, req_dev)]
        wide = jnp.concatenate(
            [jnp.where(key_head == k, q, jnp.zeros_like(q)) for k in range(KV_HEADS)], axis=1
        )
        score = lax.dot_general(
            wide, kbuf[p], (((1,), (1,)), ((), ())), preferred_element_type=jnp.float32
        ) * HEAD_DIM ** (-0.5)
        live = lax.broadcasted_iota(jnp.int32, score.shape, 1) < fill_ref[p]
        top = jnp.max(jnp.where(live, score, FLOOR), axis=1, keepdims=True)
        weight = jnp.where(live, jnp.exp(score - top), 0.0).astype(jnp.bfloat16)
        total = jnp.sum(weight.astype(jnp.float32), axis=1, keepdims=True)
        mixed = jnp.dot(weight, vbuf[p], preferred_element_type=jnp.float32)
        out = jnp.zeros(flat, jnp.float32)
        for k in range(KV_HEADS):
            out = jnp.where(key_head == k, mixed[:, k * HEAD_DIM:(k + 1) * HEAD_DIM], out)
        acc[p] = out
        maxes.append(jnp.broadcast_to(top, flat))
        sums.append(jnp.broadcast_to(total, flat))

    packed = jnp.zeros(flat, jnp.float32)
    for p in range(pages):
        same = [req_ref[p] == req_ref[q] for q in range(pages)]
        slot_max = jnp.full(flat, FLOOR, jnp.float32)
        for q in range(pages):
            slot_max = jnp.maximum(slot_max, jnp.where(same[q], maxes[q], FLOOR))
        slot_sum = jnp.zeros(flat, jnp.float32)
        slot_acc = jnp.zeros(flat, jnp.float32)
        for q in range(pages):
            factor = jnp.where(same[q], jnp.exp(maxes[q] - slot_max), 0.0)
            slot_sum += factor * sums[q]
            slot_acc += factor * acc[q]
        pbuf[p] = (slot_acc / jnp.maximum(slot_sum, 1.0)).astype(jnp.bfloat16)
        packed = jnp.where(lane == 2 * p, slot_max, packed)
        packed = jnp.where(lane == 2 * p + 1, slot_sum, packed)
    pbuf[pages] = jnp.zeros(flat, jnp.bfloat16)
    turned = jnp.concatenate(
        [packed, jnp.zeros((HEAD_DIM - heads, HEAD_DIM), jnp.float32)], axis=0
    ).T
    row = lax.broadcasted_iota(jnp.int32, (8, HEAD_DIM), 0)
    part = lax.rem(row, 4)
    for p in range(pages):
        local = lax.rem(req_ref[p], req_dev).astype(jnp.float32)
        tile = jnp.where(part == 0, turned[2 * p:2 * p + 1], turned[2 * p + 1:2 * p + 2])
        stat[p] = jnp.where(part >= 2, local, tile)
    stat[pages] = jnp.where(part == 0, FLOOR, jnp.where(part == 1, 0.0, -1.0))

    def build(g, _):
        first = leaders[SLOTS * g]
        second = leaders[SLOTS * g + 1]
        sstat[g] = jnp.where(row < 4, stat[first], stat[second])
        sdata[g, 0] = pbuf[first]
        sdata[g, 1] = pbuf[second]
        return 0

    lax.fori_loop(0, n, build, 0)

    def stat_copy(owner, peer):
        return remote(sstat.at[peer], rstat.at[owner], s_send.at[peer], s_recv.at[owner], peer)

    def data_copy(owner, peer):
        return remote(sdata.at[peer], rdata.at[owner], d_send.at[peer], d_recv.at[owner], peer)

    def send_stat(d, _):
        stat_copy(me, lax.rem(me + d, n)).start()
        return 0

    def send_data(d, _):
        data_copy(me, lax.rem(me + d, n)).start()
        return 0

    lax.fori_loop(1, n, send_stat, 0)
    lax.fori_loop(1, n, send_data, 0)
    rstat[me] = sstat[me]
    rdata[me] = sdata[me]

    def wait_stat(d, _):
        owner = lax.rem(me + n - d, n)
        stat_copy(owner, owner).wait_recv()
        return 0

    lax.fori_loop(1, n, wait_stat, 0)

    rows = 8 * n
    got = rstat[...].reshape(rows, HEAD_DIM)
    got_sum = pltpu.roll(got, rows - 1, 0)
    got_id = pltpu.roll(got, rows - 2, 0)
    got_part = lax.rem(lax.broadcasted_iota(jnp.int32, got.shape, 0), 4)
    real = got_part == 0
    ids = jnp.where(real, got_id, -1.0)
    level = jnp.zeros_like(got)
    for r in range(req_dev):
        hit = ids == r
        best = jnp.max(jnp.where(hit, got, FLOOR), axis=0, keepdims=True)
        level = jnp.where(hit, best, level)
    share = jnp.where(ids >= 0.0, got_sum * jnp.exp(jnp.minimum(got - level, 0.0)), 0.0)
    whole = jnp.ones_like(got)
    for r in range(req_dev):
        hit = ids == r
        denom = jnp.sum(jnp.where(hit, share, 0.0), axis=0, keepdims=True)
        whole = jnp.where(hit, denom, whole)
    table = jnp.where(real, share / whole, got).T[:heads]

    def wait_data(d, _):
        owner = lax.rem(me + n - d, n)
        data_copy(owner, owner).wait_recv()
        return 0

    lax.fori_loop(1, n, wait_data, 0)
    totals = [jnp.zeros((heads // 8, 8, HEAD_DIM), jnp.float32) for _ in range(req_dev)]
    for s in range(n):
        for j in range(SLOTS):
            at = 8 * s + 4 * j
            weight = jnp.broadcast_to(table[:, at:at + 1], flat)
            ident = jnp.broadcast_to(table[:8, at + 2:at + 3], (8, HEAD_DIM))
            term = (weight * rdata[s, j].astype(jnp.float32)).reshape(heads // 8, 8, HEAD_DIM)
            for r in range(req_dev):
                totals[r] += jnp.where((ident == r)[None], term, 0.0)
    rows_out = jnp.concatenate([t.reshape((1,) + flat) for t in totals], axis=0)
    o_ref[...] = rows_out.reshape(req_dev, width).astype(jnp.bfloat16)

    def done_far(k, _):
        far_copy(k, me, sibling).wait_send()
        pair_copy(k, me).wait_send()
        return 0

    lax.fori_loop(1, far_n, done_far, 0)
    pair_copy(0, me).wait_send()

    def done_sib(k, _):
        sib_copy(k, me).wait_send()
        return 0

    lax.fori_loop(0, n // 2, done_sib, 0)

    def done_out(d, _):
        peer = lax.rem(me + d, n)
        stat_copy(me, peer).wait_send()
        data_copy(me, peer).wait_send()
        return 0

    lax.fori_loop(1, n, done_out, 0)


def body(n, queries, keys, values, page_request, page_fill):
    req_dev, width = queries.shape
    pages, page_len, kv_width = keys.shape
    heads = width // HEAD_DIM
    row = (heads, HEAD_DIM)
    dma = pltpu.SemaphoreType.DMA
    smem = pl.BlockSpec(memory_space=pltpu.SMEM)
    vmem = pl.BlockSpec(memory_space=pltpu.VMEM)
    hbm = pl.BlockSpec(memory_space=pl.ANY)
    out = pl.pallas_call(
        functools.partial(kernel, n),
        out_shape=jax.ShapeDtypeStruct((req_dev, width), jnp.bfloat16),
        in_specs=[smem, smem, vmem, hbm, hbm],
        out_specs=vmem,
        scratch_shapes=[
            pltpu.VMEM((pages, page_len, kv_width), jnp.bfloat16),
            pltpu.VMEM((pages, page_len, kv_width), jnp.bfloat16),
            pltpu.VMEM((n, req_dev) + row, jnp.bfloat16),
            pltpu.VMEM((pages,) + row, jnp.float32),
            pltpu.VMEM((pages + 1,) + row, jnp.bfloat16),
            pltpu.VMEM((pages + 1, 8, HEAD_DIM), jnp.float32),
            pltpu.VMEM((n, SLOTS) + row, jnp.bfloat16),
            pltpu.VMEM((n, 8, HEAD_DIM), jnp.float32),
            pltpu.VMEM((n, SLOTS) + row, jnp.bfloat16),
            pltpu.VMEM((n, 8, HEAD_DIM), jnp.float32),
            pltpu.SMEM((SLOTS * n,), jnp.int32),
            dma((pages,)), dma((pages,)), dma((n,)), dma((n // 4,)), dma((n // 4,)),
            dma((n // 2,)), dma((n,)), dma((n,)), dma((n,)), dma((n,)),
        ],
        compiler_params=pltpu.CompilerParams(collective_id=0, has_side_effects=True),
    )(page_request, page_fill, queries, keys, values)
    return out


def solution(mesh):
    rows = P(("cell", "seq"))
    return jax.shard_map(
        functools.partial(body, mesh.shape["seq"]), mesh=mesh,
        in_specs=(rows, rows, rows, rows, rows), out_specs=rows, check_vma=False,
    )
```

```python
import functools

import jax
import jax.numpy as jnp
from jax import lax
from jax.experimental import pallas as pl
from jax.experimental.pallas import tpu as pltpu
from jax.sharding import PartitionSpec as P

HEAD_DIM = 128
KV_HEADS = 8
FLOOR = -30000.0
SLOTS = 2


def kernel(
    n, req_ref, fill_ref, q_ref, k_hbm, v_hbm, o_ref,
    kbuf, vbuf, qbuf, acc, pbuf, stat, sdata, sstat, rdata, rstat, leaders,
    k_sem, v_sem, q_recv, q_far, q_pair, q_sib, d_send, d_recv, s_send, s_recv,
):
    pages = k_hbm.shape[0]
    req_dev, width = q_ref.shape
    heads = width // HEAD_DIM
    group = heads // KV_HEADS
    far_n = n // 4
    me = lax.axis_index("seq")

    def remote(src, dst, send, recv, peer):
        return pltpu.make_async_remote_copy(
            src_ref=src, dst_ref=dst, send_sem=send, recv_sem=recv,
            device_id={"seq": peer}, device_id_type=pl.DeviceIdType.MESH,
        )

    barrier = pltpu.get_barrier_semaphore()

    far = me // 4
    place = lax.rem(me, 4)
    other = lax.rem(place + 2, 4)
    pair = far * 4 + other
    sibling = me + 1 - 2 * lax.rem(me, 2)

    def greet(peer):
        pl.semaphore_signal(
            barrier, inc=1, device_id={"seq": peer}, device_id_type=pl.DeviceIdType.MESH
        )

    def greet_far(k, _):
        greet(lax.rem(far + k, far_n) * 4 + place)
        return 0

    lax.fori_loop(1, far_n, greet_far, 0)
    greet(pair)
    greet(sibling)
    for p in range(pages):
        pltpu.make_async_copy(k_hbm.at[p], kbuf.at[p], k_sem.at[p]).start()
    for p in range(pages):
        pltpu.make_async_copy(v_hbm.at[p], vbuf.at[p], v_sem.at[p]).start()

    mine = q_ref[...].astype(jnp.float32)
    qbuf[me] = mine.reshape(req_dev, heads, HEAD_DIM).astype(jnp.bfloat16)
    pl.semaphore_wait(barrier, far_n + 1)

    def far_copy(k, owner, peer):
        return remote(qbuf.at[owner], qbuf.at[owner], q_far.at[k], q_recv.at[owner], peer)

    def pair_copy(k, owner):
        return remote(qbuf.at[owner], qbuf.at[owner], q_pair.at[k], q_recv.at[owner], pair)

    def sib_copy(k, owner):
        return remote(qbuf.at[owner], qbuf.at[owner], q_sib.at[k], q_recv.at[owner], sibling)

    def start_far(k, _):
        far_copy(k, me, lax.rem(far + k, far_n) * 4 + place).start()
        return 0

    lax.fori_loop(1, far_n, start_far, 0)
    pair_copy(0, me).start()
    sib_copy(0, me).start()

    def lead(g, _):
        first = jnp.int32(pages)
        held = jnp.int32(-1)
        for p in reversed(range(pages)):
            hit = req_ref[p] // req_dev == g
            first = jnp.where(hit, p, first)
            held = jnp.where(hit, req_ref[p], held)
        second = jnp.int32(pages)
        for p in reversed(range(pages)):
            hit = jnp.logical_and(req_ref[p] // req_dev == g, req_ref[p] != held)
            second = jnp.where(hit, p, second)
        leaders[SLOTS * g] = first
        leaders[SLOTS * g + 1] = second
        return 0

    lax.fori_loop(0, n, lead, 0)

    def pass_far(k, _):
        owner = lax.rem(far + far_n - k, far_n) * 4 + place
        far_copy(k, owner, owner).wait_recv()
        pair_copy(k, owner).start()
        sib_copy(k, owner).start()
        return 0

    lax.fori_loop(1, far_n, pass_far, 0)

    def pass_pair(k, _):
        owner = lax.rem(far + far_n - k, far_n) * 4 + other
        pair_copy(k, owner).wait_recv()
        sib_copy(far_n + k, owner).start()
        return 0

    lax.fori_loop(0, far_n, pass_pair, 0)

    def wait_sib(k, _):
        owner = 2 * k + lax.rem(sibling, 2)
        sib_copy(k, owner).wait_recv()
        return 0

    lax.fori_loop(0, n // 2, wait_sib, 0)

    for p in range(pages):
        pltpu.make_async_copy(k_hbm.at[p], kbuf.at[p], k_sem.at[p]).wait()
        pltpu.make_async_copy(v_hbm.at[p], vbuf.at[p], v_sem.at[p]).wait()
    lane = lax.broadcasted_iota(jnp.int32, (heads, HEAD_DIM), 1)
    key_head = lax.broadcasted_iota(jnp.int32, (heads, HEAD_DIM), 0) // group
    flat = (heads, HEAD_DIM)
    maxes, sums = [], []
    for p in range(pages):
        r = req_ref[p]
        q = qbuf[r // req_dev, lax.rem(r, req_dev)]
        wide = jnp.concatenate(
            [jnp.where(key_head == k, q, jnp.zeros_like(q)) for k in range(KV_HEADS)], axis=1
        )
        score = lax.dot_general(
            wide, kbuf[p], (((1,), (1,)), ((), ())), preferred_element_type=jnp.float32
        ) * HEAD_DIM ** (-0.5)
        live = lax.broadcasted_iota(jnp.int32, score.shape, 1) < fill_ref[p]
        top = jnp.max(jnp.where(live, score, FLOOR), axis=1, keepdims=True)
        weight = jnp.where(live, jnp.exp(score - top), 0.0).astype(jnp.bfloat16)
        total = jnp.sum(weight.astype(jnp.float32), axis=1, keepdims=True)
        mixed = jnp.dot(weight, vbuf[p], preferred_element_type=jnp.float32)
        out = jnp.zeros(flat, jnp.float32)
        for k in range(KV_HEADS):
            out = jnp.where(key_head == k, mixed[:, k * HEAD_DIM:(k + 1) * HEAD_DIM], out)
        acc[p] = out
        maxes.append(jnp.broadcast_to(top, flat))
        sums.append(jnp.broadcast_to(total, flat))

    packed = jnp.zeros(flat, jnp.float32)
    for p in range(pages):
        same = [req_ref[p] == req_ref[q] for q in range(pages)]
        slot_max = jnp.full(flat, FLOOR, jnp.float32)
        for q in range(pages):
            slot_max = jnp.maximum(slot_max, jnp.where(same[q], maxes[q], FLOOR))
        slot_sum = jnp.zeros(flat, jnp.float32)
        slot_acc = jnp.zeros(flat, jnp.float32)
        for q in range(pages):
            factor = jnp.where(same[q], jnp.exp(maxes[q] - slot_max), 0.0)
            slot_sum += factor * sums[q]
            slot_acc += factor * acc[q]
        pbuf[p] = (slot_acc / jnp.maximum(slot_sum, 1.0)).astype(jnp.bfloat16)
        packed = jnp.where(lane == 2 * p, slot_max, packed)
        packed = jnp.where(lane == 2 * p + 1, slot_sum, packed)
    pbuf[pages] = jnp.zeros(flat, jnp.bfloat16)
    turned = jnp.concatenate(
        [packed, jnp.zeros((HEAD_DIM - heads, HEAD_DIM), jnp.float32)], axis=0
    ).T
    row = lax.broadcasted_iota(jnp.int32, (8, HEAD_DIM), 0)
    part = lax.rem(row, 4)
    for p in range(pages):
        local = lax.rem(req_ref[p], req_dev).astype(jnp.float32)
        tile = jnp.where(part == 0, turned[2 * p:2 * p + 1], turned[2 * p + 1:2 * p + 2])
        stat[p] = jnp.where(part >= 2, local, tile)
    stat[pages] = jnp.where(part == 0, FLOOR, jnp.where(part == 1, 0.0, -1.0))

    def build(g, _):
        first = leaders[SLOTS * g]
        second = leaders[SLOTS * g + 1]
        sstat[g] = jnp.where(row < 4, stat[first], stat[second])
        sdata[g, 0] = pbuf[first]
        sdata[g, 1] = pbuf[second]
        return 0

    lax.fori_loop(0, n, build, 0, unroll=4)

    def stat_copy(owner, peer):
        return remote(sstat.at[peer], rstat.at[owner], s_send.at[peer], s_recv.at[owner], peer)

    def data_copy(owner, peer):
        return remote(sdata.at[peer], rdata.at[owner], d_send.at[peer], d_recv.at[owner], peer)

    def send_stat(d, _):
        stat_copy(me, lax.rem(me + d, n)).start()
        return 0

    def send_data(d, _):
        data_copy(me, lax.rem(me + d, n)).start()
        return 0

    lax.fori_loop(1, n, send_stat, 0)
    lax.fori_loop(1, n, send_data, 0)
    rstat[me] = sstat[me]
    rdata[me] = sdata[me]

    def wait_stat(d, _):
        owner = lax.rem(me + n - d, n)
        stat_copy(owner, owner).wait_recv()
        return 0

    lax.fori_loop(1, n, wait_stat, 0)

    rows = 8 * n
    got = rstat[...].reshape(rows, HEAD_DIM)
    got_sum = pltpu.roll(got, rows - 1, 0)
    got_id = pltpu.roll(got, rows - 2, 0)
    got_part = lax.rem(lax.broadcasted_iota(jnp.int32, got.shape, 0), 4)
    real = got_part == 0
    ids = jnp.where(real, got_id, -1.0)
    level = jnp.zeros_like(got)
    for r in range(req_dev):
        hit = ids == r
        best = jnp.max(jnp.where(hit, got, FLOOR), axis=0, keepdims=True)
        level = jnp.where(hit, best, level)
    share = jnp.where(ids >= 0.0, got_sum * jnp.exp(jnp.minimum(got - level, 0.0)), 0.0)
    whole = jnp.ones_like(got)
    for r in range(req_dev):
        hit = ids == r
        denom = jnp.sum(jnp.where(hit, share, 0.0), axis=0, keepdims=True)
        whole = jnp.where(hit, denom, whole)
    table = jnp.where(real, share / whole, got).T[:heads]

    def wait_data(d, _):
        owner = lax.rem(me + n - d, n)
        data_copy(owner, owner).wait_recv()
        return 0

    lax.fori_loop(1, n, wait_data, 0)
    totals = [jnp.zeros((heads // 8, 8, HEAD_DIM), jnp.float32) for _ in range(req_dev)]
    for s in range(n):
        for j in range(SLOTS):
            at = 8 * s + 4 * j
            weight = jnp.broadcast_to(table[:, at:at + 1], flat)
            ident = jnp.broadcast_to(table[:8, at + 2:at + 3], (8, HEAD_DIM))
            term = (weight * rdata[s, j].astype(jnp.float32)).reshape(heads // 8, 8, HEAD_DIM)
            for r in range(req_dev):
                totals[r] += jnp.where((ident == r)[None], term, 0.0)
    for r in range(req_dev):
        o_ref[r] = totals[r].reshape(flat).astype(jnp.bfloat16)

    def done_far(k, _):
        far_copy(k, me, sibling).wait_send()
        pair_copy(k, me).wait_send()
        return 0

    lax.fori_loop(1, far_n, done_far, 0)
    pair_copy(0, me).wait_send()

    def done_sib(k, _):
        sib_copy(k, me).wait_send()
        return 0

    lax.fori_loop(0, n // 2, done_sib, 0)

    def done_out(d, _):
        peer = lax.rem(me + d, n)
        stat_copy(me, peer).wait_send()
        data_copy(me, peer).wait_send()
        return 0

    lax.fori_loop(1, n, done_out, 0)


def body(n, queries, keys, values, page_request, page_fill):
    req_dev, width = queries.shape
    pages, page_len, kv_width = keys.shape
    heads = width // HEAD_DIM
    row = (heads, HEAD_DIM)
    dma = pltpu.SemaphoreType.DMA
    smem = pl.BlockSpec(memory_space=pltpu.SMEM)
    vmem = pl.BlockSpec(memory_space=pltpu.VMEM)
    hbm = pl.BlockSpec(memory_space=pl.ANY)
    out = pl.pallas_call(
        functools.partial(kernel, n),
        out_shape=jax.ShapeDtypeStruct((req_dev,) + row, jnp.bfloat16),
        in_specs=[smem, smem, vmem, hbm, hbm],
        out_specs=vmem,
        scratch_shapes=[
            pltpu.VMEM((pages, page_len, kv_width), jnp.bfloat16),
            pltpu.VMEM((pages, page_len, kv_width), jnp.bfloat16),
            pltpu.VMEM((n, req_dev) + row, jnp.bfloat16),
            pltpu.VMEM((pages,) + row, jnp.float32),
            pltpu.VMEM((pages + 1,) + row, jnp.bfloat16),
            pltpu.VMEM((pages + 1, 8, HEAD_DIM), jnp.float32),
            pltpu.VMEM((n, SLOTS) + row, jnp.bfloat16),
            pltpu.VMEM((n, 8, HEAD_DIM), jnp.float32),
            pltpu.VMEM((n, SLOTS) + row, jnp.bfloat16),
            pltpu.VMEM((n, 8, HEAD_DIM), jnp.float32),
            pltpu.SMEM((SLOTS * n,), jnp.int32),
            dma((pages,)), dma((pages,)), dma((n,)), dma((n // 4,)), dma((n // 4,)),
            dma((n // 2,)), dma((n,)), dma((n,)), dma((n,)), dma((n,)),
        ],
        compiler_params=pltpu.CompilerParams(collective_id=0, has_side_effects=True),
    )(page_request, page_fill, queries, keys, values)
    return out.reshape(req_dev, width)


def solution(mesh):
    rows = P(("cell", "seq"))
    return jax.shard_map(
        functools.partial(body, mesh.shape["seq"]), mesh=mesh,
        in_specs=(rows, rows, rows, rows, rows), out_specs=rows, check_vma=False,
    )
```
